32 devices in a mesh: groups: 2 (over y), tile: 16 (over z, x, core).
Axes of the slice: x: 2, y: 2, z: 4, core: 2. Of those that a mesh axis runs over, the one named last changes fastest.
Arguments:
- fine: bfloat16 [64, 256, 256], P(('groups', 'tile')), parts along dimension 0, may hold values from -12 to 12
- conv_weight: bfloat16 [3, 3, 256, 256], replicated, may hold values from -0.125 to 0.125
- qk_weight: bfloat16 [2, 256, 128], replicated, may hold values from -2 to 2
- v_weight: bfloat16 [256, 128], replicated, may hold values from -0.375 to 0.375
- o_weight: bfloat16 [128, 256], replicated, may hold values from -0.5 to 0.5
- upstream: bfloat16 [4096, 256], P(('groups', 'tile')), parts along dimension 0, may hold values from -6 to 6
Outputs:
- block_out: bfloat16 [4096, 256], P(('groups', 'tile')), parts along dimension 0
- grad_conv: float32 [6, 3, 256, 256], P('groups'), parts along dimension 0
- grad_fine: bfloat16 [64, 256, 256], P(('groups', 'tile')), parts along dimension 0
The draws below stay inside these ranges and needn't reach their ends.
There are 2 independent parts, one for each index of `groups`. The reference program is written for one: setup_inputs(seed, part) draws one part's arguments, and reference() takes and returns one part's arrays. A program takes and returns all parts, laid end to end along the dimension named above; an argument that names none is the same for every part. Nothing has to cross between parts.
All inputs are finite; a program needn't handle non-finite values.
Results may differ from the reference program's by a relative error of at most 0.035.
The reference program's roundings to bfloat16 on the way count: a program that leaves them out, or rounds other values in their place, can miss the bound.
Values may be sent and summed in bfloat16 or wider, within the bound.
A program may use at most 64 MiB of HBM per device.

```python
import math
import jax
import jax.numpy as jnp
from jax import lax

C = 256
HEADS = 2
HDIM = 64
WC = 128
HD = 128
ROWS = 16
FROWS = 32
FCOLS = 256
TOKENS = 2048


def draw_fine(key, part):
    base = jnp.clip(jax.random.normal(key, (FROWS, FCOLS, C), jnp.float32), -4.0, 4.0)
    return base.astype(jnp.bfloat16)


def draw_qk_weight(key, part):
    first = jax.random.normal(jax.random.fold_in(key, 1), (C, HD), jnp.float32)
    second = jax.random.normal(jax.random.fold_in(key, 2), (C, HD), jnp.float32)
    stacked = jnp.clip(jnp.stack([first, second]), -5.0, 5.0) * (1.7 / math.sqrt(C))
    return stacked.astype(jnp.bfloat16)


def level_of(own_key, dims, shards, smallest, largest):
    level = 1.0
    for axis_at, parts in shards:
        heights = jax.random.uniform(jax.random.fold_in(jax.random.fold_in(own_key, 6), axis_at), (parts,), jnp.float32, smallest / len(shards), largest / len(shards))
        level = level * jnp.repeat(jnp.exp(heights), dims[axis_at] // parts).reshape((-1,) + (1,) * (len(dims) - 1 - axis_at))
    return level


def noise(key, extent, width, reach, cuts=(), kind=jnp.bfloat16):
    entries = jax.random.normal(key, extent, jnp.float32) * width
    if len(cuts) > 0:
        entries = level_of(key, extent, cuts, -0.22, 0.18) * entries
    return jnp.clip(entries, min=-reach, max=reach).astype(kind)


def setup_inputs(seed: int = 0, part: int = 0) -> dict:
    streams_of = jax.random.split(jax.random.key(seed), 7)
    part_keys = jax.random.split(jax.random.fold_in(streams_of[6], part), 7)
    return {
        "fine": draw_fine(jax.random.fold_in(jax.random.fold_in(streams_of[6], part), 71), part),
        "conv_weight": noise(streams_of[1], (3, 3, C, C), (9 * C) ** -0.5, 0.125),
        "qk_weight": draw_qk_weight(jax.random.fold_in(streams_of[6], 71), part),
        "v_weight": noise(streams_of[3], (C, HD), C ** -0.5, 0.375),
        "o_weight": noise(streams_of[4], (HD, C), HD ** -0.5, 0.5),
        "upstream": noise(part_keys[5], (TOKENS, C), 1.0, 6.0, ((0, 16),)),
    }


def conv_taps(fine):
    padded = jnp.pad(fine, ((1, 0), (1, 0), (0, 0)))
    taps = []
    for a in range(3):
        for b in range(3):
            taps.append(padded[a:a + 2 * ROWS:2, b:b + 2 * WC:2].reshape(ROWS * WC, C))
    return taps

def split_heads(mat):
    return mat.reshape(mat.shape[0], HEADS, HDIM).transpose(1, 0, 2).astype(jnp.float32)

def join_heads(mat):
    return mat.transpose(1, 0, 2).reshape(mat.shape[1], HD)

def reference(fine, conv_weight, qk_weight, v_weight, o_weight, upstream):
    taps = conv_taps(fine)
    total = jnp.zeros((TOKENS, C), jnp.float32)
    for a in range(3):
        for b in range(3):
            total = total + jnp.dot(taps[3 * a + b], conv_weight[a, b], preferred_element_type=jnp.float32)
    hidden = total.astype(jnp.bfloat16)
    query = jnp.dot(hidden, qk_weight[0], preferred_element_type=jnp.float32).astype(jnp.bfloat16)
    keys = jnp.dot(hidden, qk_weight[1], preferred_element_type=jnp.float32).astype(jnp.bfloat16)
    values = jnp.dot(hidden, v_weight, preferred_element_type=jnp.float32).astype(jnp.bfloat16)
    q_heads = split_heads(query)
    k_heads = split_heads(keys)
    v_heads = split_heads(values)
    scale = HDIM ** (-0.5)
    block = math.gcd(TOKENS, 1024)
    count = TOKENS // block

    def forward_block(index):
        q_part = lax.dynamic_slice_in_dim(q_heads, index * block, block, 1)
        scores = jnp.einsum('hqd,hkd->hqk', q_part, k_heads) * scale
        top = lax.optimization_barrier(jnp.max(scores, axis=2, keepdims=True))
        lse = top + jnp.log(lax.optimization_barrier(jnp.sum(jnp.exp(scores - top), axis=2, keepdims=True)))
        prob = jnp.exp(scores - lse).astype(jnp.bfloat16).astype(jnp.float32)
        return (jnp.einsum('hqk,hkd->hqd', prob, v_heads), lse[:, :, 0])
    out_blocks, lse_blocks = lax.map(forward_block, jnp.arange(count, dtype=jnp.int32))
    attended = join_heads(out_blocks.transpose(1, 0, 2, 3).reshape(HEADS, TOKENS, HDIM)).astype(jnp.bfloat16)
    lse = lse_blocks.transpose(1, 0, 2).reshape(HEADS, TOKENS)
    block_out = (hidden.astype(jnp.float32) + jnp.dot(attended, o_weight, preferred_element_type=jnp.float32)).astype(jnp.bfloat16)
    dattended = jnp.dot(upstream, o_weight.T, preferred_element_type=jnp.float32).astype(jnp.bfloat16)
    d_heads = split_heads(dattended)
    a_heads = split_heads(attended)
    delta = lax.optimization_barrier(jnp.sum(d_heads * a_heads, axis=2))

    def query_block(index):
        q_part = lax.dynamic_slice_in_dim(q_heads, index * block, block, 1)
        d_part = lax.dynamic_slice_in_dim(d_heads, index * block, block, 1)
        l_part = lax.dynamic_slice_in_dim(lse, index * block, block, 1)
        e_part = lax.dynamic_slice_in_dim(delta, index * block, block, 1)
        scores = jnp.einsum('hqd,hkd->hqk', q_part, k_heads) * scale
        prob = jnp.exp(scores - l_part[:, :, None])
        dprob = jnp.einsum('hqd,hkd->hqk', d_part, v_heads)
        dscore = (prob * (dprob - e_part[:, :, None]) * scale).astype(jnp.bfloat16).astype(jnp.float32)
        return jnp.einsum('hqk,hkd->hqd', dscore, k_heads)

    def key_block(index):
        k_part = lax.dynamic_slice_in_dim(k_heads, index * block, block, 1)
        v_part = lax.dynamic_slice_in_dim(v_heads, index * block, block, 1)
        scores = jnp.einsum('hqd,hkd->hqk', q_heads, k_part) * scale
        prob = jnp.exp(scores - lse[:, :, None])
        prob_low = prob.astype(jnp.bfloat16).astype(jnp.float32)
        dvals = jnp.einsum('hqk,hqd->hkd', prob_low, d_heads)
        dprob = jnp.einsum('hqd,hkd->hqk', d_heads, v_part)
        dscore = (prob * (dprob - delta[:, :, None]) * scale).astype(jnp.bfloat16).astype(jnp.float32)
        dkeys = jnp.einsum('hqk,hqd->hkd', dscore, q_heads)
        return (dkeys, dvals)
    dq_blocks = lax.map(query_block, jnp.arange(count, dtype=jnp.int32))
    dk_blocks, dv_blocks = lax.map(key_block, jnp.arange(count, dtype=jnp.int32))

    def gather_blocks(blocks):
        return join_heads(blocks.transpose(1, 0, 2, 3).reshape(HEADS, TOKENS, HDIM)).astype(jnp.bfloat16)
    dquery = gather_blocks(dq_blocks)
    dkeys = gather_blocks(dk_blocks)
    dvalues = gather_blocks(dv_blocks)
    dhidden = upstream.astype(jnp.float32)
    dhidden = dhidden + jnp.dot(dquery, qk_weight[0].T, preferred_element_type=jnp.float32)
    dhidden = dhidden + jnp.dot(dkeys, qk_weight[1].T, preferred_element_type=jnp.float32)
    dhidden = dhidden + jnp.dot(dvalues, v_weight.T, preferred_element_type=jnp.float32)
    dhidden = dhidden.astype(jnp.bfloat16)
    kernel_rows = []
    dpadded = jnp.zeros((2 * ROWS + 1, 2 * WC + 1, C), jnp.float32)
    for a in range(3):
        row_list = []
        for b in range(3):
            row_list.append(jnp.dot(taps[3 * a + b].T, dhidden, preferred_element_type=jnp.float32))
            back = jnp.dot(dhidden, conv_weight[a, b].T, preferred_element_type=jnp.float32)
            dpadded = dpadded.at[a:a + 2 * ROWS:2, b:b + 2 * WC:2].add(back.reshape(ROWS, WC, C))
        kernel_rows.append(jnp.stack(row_list))
    grad_conv = jnp.stack(kernel_rows) * (1.0 / math.sqrt(TOKENS))
    grad_fine = dpadded[1:, 1:].astype(jnp.bfloat16)
    return (block_out, grad_conv, grad_fine)
```

```python
import functools
import math

import jax
import jax.numpy as jnp
from jax import lax
from jax.experimental import pallas as pl
from jax.experimental.pallas import tpu as pltpu
from jax.sharding import PartitionSpec as P

HEADS = 2
HDIM = 64
HD = 128


def shifted(x, axis, by):
    peers = lax.axis_size(axis)
    pairs = [(i, i + by) for i in range(peers) if 0 <= i + by < peers]
    return lax.ppermute(x, axis, pairs)


def head_view(mat):
    return mat.reshape(mat.shape[0], HEADS, HDIM)


def score_block(queries, keys):
    product = jnp.einsum(
        "qhd,khd->hqk", head_view(queries), head_view(keys), preferred_element_type=jnp.float32
    )
    return product * HDIM ** (-0.5)


def dot_back(left, right):
    return lax.dot_general(
        left, right, (((1,), (1,)), ((), ())), preferred_element_type=jnp.float32
    )


def dot_over(left, right):
    return lax.dot_general(
        left, right, (((0,), (0,)), ((), ())), preferred_element_type=jnp.float32
    )


def body(fine, conv_weight, qk_weight, v_weight, o_weight, upstream):
    rows = fine.shape[0] // 2
    cols = fine.shape[1] // 2
    chans = fine.shape[2]
    local = rows * cols
    scale = HDIM ** (-0.5)
    above = shifted(fine[-1:], "tile", 1)
    padded = jnp.pad(jnp.concatenate([above, fine], axis=0), ((0, 0), (1, 0), (0, 0)))
    taps = []
    total = jnp.zeros((local, chans), jnp.float32)
    for a in range(3):
        for b in range(3):
            tap = padded[a : a + 2 * rows : 2, b : b + 2 * cols : 2].reshape(local, chans)
            taps.append(tap)
            total = total + jnp.dot(tap, conv_weight[a, b], preferred_element_type=jnp.float32)
    hidden = total.astype(jnp.bfloat16)
    query = jnp.dot(hidden, qk_weight[0], preferred_element_type=jnp.float32).astype(jnp.bfloat16)
    key_loc = jnp.dot(hidden, qk_weight[1], preferred_element_type=jnp.float32).astype(jnp.bfloat16)
    value_loc = jnp.dot(hidden, v_weight, preferred_element_type=jnp.float32).astype(jnp.bfloat16)
    keys_all, values_all = (
        lax.all_gather(key_loc, "tile", axis=0, tiled=True),
        lax.all_gather(value_loc, "tile", axis=0, tiled=True),
    )
    everyone = keys_all.shape[0]
    block = math.gcd(everyone, 2048)
    steps_total = everyone // block

    def stats_step(index, carry):
        top, summed = carry
        scores = score_block(query, lax.dynamic_slice_in_dim(keys_all, index * block, block, 0))
        new_top = jnp.maximum(top, jnp.max(scores, axis=2))
        summed = summed * jnp.exp(top - new_top) + jnp.sum(
            jnp.exp(scores - new_top[:, :, None]), axis=2
        )
        return (new_top, summed)

    start_top = jnp.full((HEADS, local), -jnp.inf, jnp.float32)
    top, summed = lax.fori_loop(
        0, steps_total, stats_step, (start_top, jnp.zeros((HEADS, local), jnp.float32))
    )
    lse = top + jnp.log(summed)

    def value_step(index, acc):
        scores = score_block(query, lax.dynamic_slice_in_dim(keys_all, index * block, block, 0))
        weights = jnp.exp(scores - lse[:, :, None]).astype(jnp.bfloat16)
        v_part = head_view(lax.dynamic_slice_in_dim(values_all, index * block, block, 0))
        return acc + jnp.einsum("hqk,khd->qhd", weights, v_part, preferred_element_type=jnp.float32)

    mixed = lax.fori_loop(0, steps_total, value_step, jnp.zeros((local, HEADS, HDIM), jnp.float32))
    attended = mixed.reshape(local, HD).astype(jnp.bfloat16)
    block_out = (
        hidden.astype(jnp.float32) + jnp.dot(attended, o_weight, preferred_element_type=jnp.float32)
    ).astype(jnp.bfloat16)
    dattended = dot_back(upstream, o_weight).astype(jnp.bfloat16)
    product = dattended.astype(jnp.float32) * attended.astype(jnp.float32)
    delta = jnp.sum(product.reshape(local, HEADS, HDIM), axis=2).T

    def query_step(index, acc):
        k_part = lax.dynamic_slice_in_dim(keys_all, index * block, block, 0)
        v_part = lax.dynamic_slice_in_dim(values_all, index * block, block, 0)
        prob = jnp.exp(score_block(query, k_part) - lse[:, :, None])
        dprob = jnp.einsum(
            "qhd,khd->hqk",
            head_view(dattended),
            head_view(v_part),
            preferred_element_type=jnp.float32,
        )
        dscore = (prob * (dprob - delta[:, :, None]) * scale).astype(jnp.bfloat16)
        return acc + jnp.einsum(
            "hqk,khd->qhd", dscore, head_view(k_part), preferred_element_type=jnp.float32
        )

    dq_acc = lax.fori_loop(0, steps_total, query_step, jnp.zeros((local, HEADS, HDIM), jnp.float32))
    dquery = dq_acc.reshape(local, HD).astype(jnp.bfloat16)
    lse_all, delta_all = (
        lax.all_gather(lse.T, "tile", axis=0, tiled=True),
        lax.all_gather(delta.T, "tile", axis=0, tiled=True),
    )
    empty = jnp.zeros((local, HEADS, HDIM), jnp.float32)
    q_in = lax.all_gather(query, "tile", axis=0, tiled=True)
    d_in = lax.all_gather(dattended, "tile", axis=0, tiled=True)
    incoming = q_in.shape[0]
    sub = math.gcd(incoming, 2048)

    def inner(index, acc):
        dk_acc, dv_acc = acc
        at = index * sub
        q_part = lax.dynamic_slice_in_dim(q_in, at, sub, 0)
        d_part = lax.dynamic_slice_in_dim(d_in, at, sub, 0)
        l_part = lax.dynamic_slice_in_dim(lse_all, at, sub, 0).T
        e_part = lax.dynamic_slice_in_dim(delta_all, at, sub, 0).T
        prob = jnp.exp(score_block(q_part, key_loc) - l_part[:, :, None])
        dv_acc = dv_acc + jnp.einsum(
            "hqk,qhd->khd",
            prob.astype(jnp.bfloat16),
            head_view(d_part),
            preferred_element_type=jnp.float32,
        )
        dprob = jnp.einsum(
            "qhd,khd->hqk",
            head_view(d_part),
            head_view(value_loc),
            preferred_element_type=jnp.float32,
        )
        dscore = (prob * (dprob - e_part[:, :, None]) * scale).astype(jnp.bfloat16)
        dk_acc = dk_acc + jnp.einsum(
            "hqk,qhd->khd", dscore, head_view(q_part), preferred_element_type=jnp.float32
        )
        return (dk_acc, dv_acc)

    dk_acc, dv_acc = lax.fori_loop(0, incoming // sub, inner, (empty, empty))
    dkeys = dk_acc.reshape(local, HD).astype(jnp.bfloat16)
    dvalues = dv_acc.reshape(local, HD).astype(jnp.bfloat16)
    dhidden = upstream.astype(jnp.float32)
    dhidden = dhidden + dot_back(dquery, qk_weight[0])
    dhidden = dhidden + dot_back(dkeys, qk_weight[1])
    dhidden = dhidden + dot_back(dvalues, v_weight)
    dhidden = dhidden.astype(jnp.bfloat16)
    kernel_rows = []
    dpadded = jnp.zeros((2 * rows + 1, 2 * cols + 1, chans), jnp.float32)
    for a in range(3):
        row_list = []
        for b in range(3):
            row_list.append(dot_over(taps[3 * a + b], dhidden))
            back = dot_back(dhidden, conv_weight[a, b])
            dpadded = dpadded.at[a : a + 2 * rows : 2, b : b + 2 * cols : 2].add(
                back.reshape(rows, cols, chans)
            )
        kernel_rows.append(jnp.stack(row_list))
    kernel_local = jnp.stack(kernel_rows)
    grad_conv = lax.psum(kernel_local, "tile") * (1.0 / math.sqrt(everyone))
    below = shifted(dpadded[0:1, 1:].astype(jnp.bfloat16), "tile", -1).astype(jnp.float32)
    grad_fine = dpadded[1:, 1:]
    grad_fine = grad_fine.at[-1:].add(below)
    return (block_out, grad_conv, grad_fine.astype(jnp.bfloat16))


NT = (((1,), (1,)), ((), ()))
NN = (((1,), (0,)), ((), ()))


def mm(left, right, dims=NN):
    return lax.dot_general(left, right, dims, preferred_element_type=jnp.float32)


def two_heads(mat):
    lane = lax.broadcasted_iota(jnp.int32, mat.shape, 1)
    zero = jnp.zeros_like(mat)
    return jnp.concatenate(
        [jnp.where(lane < HDIM, mat, zero), jnp.where(lane < HDIM, zero, mat)], axis=0
    )


def pick_heads(mat):
    half = mat.shape[0] // 2
    lane = lax.broadcasted_iota(jnp.int32, (half, mat.shape[1]), 1)
    return jnp.where(lane < HDIM, mat[:half], mat[half:])


class Gather:
    def __init__(self, view, me, peers, send, recv, slot):
        self.view, self.peers, self.send, self.recv, self.slot = view, peers, send, recv, slot
        self.zs = peers // 4
        self.core = lax.rem(me, 2)
        self.x = lax.rem(lax.div(me, 2), 2)
        self.z = lax.div(me, 4)
        self.me = me
        self.copies = []

    def at(self, dz, flip_x=0, flip_core=0):
        z = lax.rem(self.z + dz + self.zs, self.zs)
        x = 1 - self.x if flip_x else self.x
        core = 1 - self.core if flip_core else self.core
        return z * 4 + x * 2 + core

    def copy(self, index, block, target):
        return pltpu.make_async_remote_copy(
            src_ref=self.view(block),
            dst_ref=self.view(block),
            send_sem=self.send.at[self.slot, index],
            recv_sem=self.recv.at[self.slot, index],
            device_id={"tile": target},
            device_id_type=pl.DeviceIdType.MESH,
        )

    def go(self, index, block, target):
        made = self.copy(index, block, target)
        made.start()
        self.copies.append(made)

    def landed(self, index, block):
        self.copy(index, block, self.at(0, 1)).wait_recv()

    def own(self):
        zs = self.zs
        for d in range(1, zs):
            self.go(d - 1, self.me, self.at(d))
        self.go(zs - 1, self.me, self.at(0, 1))
        self.go(2 * zs - 1, self.me, self.at(0, 0, 1))

    def across(self):
        zs = self.zs
        for d in range(1, zs):
            block = self.at(-d)
            self.landed(d - 1, block)
            self.go(zs - 1 + d, block, self.at(0, 1))
            self.go(2 * zs - 1 + d, block, self.at(0, 0, 1))

    def over(self):
        zs = self.zs
        for d in range(zs):
            block = self.at(-d, 1)
            self.landed(zs - 1 + d, block)
            self.go(3 * zs - 1 + d, block, self.at(0, 0, 1))

    def finish(self):
        zs = self.zs
        for d in range(zs):
            self.landed(2 * zs - 1 + d, self.at(-d, 0, 1))
            self.landed(3 * zs - 1 + d, self.at(-d, 1, 1))

    def drain(self):
        for made in self.copies:
            made.wait_send()


def fused_kernel(
    peers,
    fine,
    conv,
    qk,
    vw,
    ow,
    up,
    block_out,
    grad_conv,
    grad_fine,
    above,
    kv_all,
    qd_all,
    dh_all,
    shift_all,
    fine_t,
    stats,
    st_buf,
    dpt_buf,
    send,
    recv,
    stat_send,
    stat_recv,
    halo_send,
    halo_recv,
):
    me = lax.axis_index("tile")
    n = up.shape[0]
    chans = up.shape[1]
    full = n * peers
    lower = lax.rem(me + 1, peers)
    upper = lax.rem(me + peers - 1, peers)

    barrier = pltpu.get_barrier_semaphore()
    for step in range(1, peers):
        pl.semaphore_signal(
            barrier,
            inc=1,
            device_id={"tile": lax.rem(me + step, peers)},
            device_id_type=pl.DeviceIdType.MESH,
        )

    def rows(ref):
        return lambda t: ref.at[pl.ds(pl.multiple_of(t * n, n), n), :]

    def cols(ref):
        return lambda t: ref.at[:, pl.ds(pl.multiple_of(t * n, n), n)]

    mine = pl.ds(pl.multiple_of(me * n, n), n)
    for r in range(2):
        fine_t[r * 2 * chans : (r + 1) * 2 * chans, mine] = fine[r].T
    pl.semaphore_wait(barrier, peers - 1)
    halo = pltpu.make_async_remote_copy(
        src_ref=fine.at[1],
        dst_ref=above,
        send_sem=halo_send,
        recv_sem=halo_recv,
        device_id={"tile": lower},
        device_id_type=pl.DeviceIdType.MESH,
    )
    halo.start()
    fine_gather = Gather(cols(fine_t), me, peers, send, recv, 0)
    kv_gather = Gather(rows(kv_all), me, peers, send, recv, 1)
    qd_gather = Gather(rows(qd_all), me, peers, send, recv, 2)
    dh_gather = Gather(rows(dh_all), me, peers, send, recv, 3)

    def conv_row(a, row):
        straight = mm(row[:, :chans], conv[a, 1]) + mm(row[:, chans:], conv[a, 2])
        return straight, mm(row[:, chans:], conv[a, 0])

    mid, mid_late = conv_row(1, fine[0])
    low, low_late = conv_row(2, fine[1])
    dattended = mm(up[...], ow[...], NT).astype(jnp.bfloat16)
    halo.wait_recv()
    top_row = jnp.where(me == 0, jnp.zeros_like(above[...]), above[...])
    top, top_late = conv_row(0, top_row)
    late = top_late + mid_late + low_late
    row_at = lax.broadcasted_iota(jnp.int32, (n, chans), 0)
    late = jnp.where(row_at == 0, 0.0, pltpu.roll(late, 1, 0))
    hidden = (top + mid + low + late).astype(jnp.bfloat16)
    keys = mm(hidden, qk[1]).astype(jnp.bfloat16)
    values = mm(hidden, vw[...]).astype(jnp.bfloat16)
    kv_all[mine, :] = jnp.concatenate([keys, values], axis=1)
    kv_gather.own()
    query = (mm(hidden, qk[0]).astype(jnp.bfloat16) * jnp.bfloat16(HDIM**-0.5)).astype(jnp.bfloat16)
    qd_all[mine, :] = jnp.concatenate([query, dattended], axis=1)
    kv_gather.across()
    kv_gather.over()
    qd_gather.own()
    kv_gather.finish()
    fine_gather.own()

    q2 = two_heads(query)
    d2 = two_heads(dattended)
    scores = mm(q2, kv_all[:, :HD], NT)
    high = jnp.max(scores, axis=1, keepdims=True)
    expd = jnp.exp(scores - high)
    total = jnp.sum(expd, axis=1, keepdims=True)
    lse = high + jnp.log(total)
    prob = expd * (1.0 / total)
    attended = pick_heads(mm(prob.astype(jnp.bfloat16), kv_all[:, HD:])).astype(jnp.bfloat16)
    product = dattended.astype(jnp.float32) * attended.astype(jnp.float32)
    delta = jnp.sum(two_heads(product), axis=1, keepdims=True)
    lane = lax.broadcasted_iota(jnp.int32, (2 * n, 128), 1)
    packed = jnp.where(lane == 0, lse, jnp.where(lane == 1, delta, 0.0)).T
    stats[me] = packed[:2]
    stat_copies = []
    for step in range(1, peers):
        made = pltpu.make_async_remote_copy(
            src_ref=stats.at[me],
            dst_ref=stats.at[me],
            send_sem=stat_send.at[step],
            recv_sem=stat_recv.at[step],
            device_id={"tile": lax.rem(me + step, peers)},
            device_id_type=pl.DeviceIdType.MESH,
        )
        made.start()
        stat_copies.append(made)
    qd_gather.across()
    qd_gather.over()
    block_out[...] = (hidden.astype(jnp.float32) + mm(attended, ow[...])).astype(jnp.bfloat16)
    dprob = mm(d2, kv_all[:, HD:], NT)
    dscore = (prob * (dprob - delta)).astype(jnp.bfloat16)
    dquery = (pick_heads(mm(dscore, kv_all[:, :HD])) * HDIM**-0.5).astype(jnp.bfloat16)
    grad_h = up[...].astype(jnp.float32) + mm(dquery, qk[0], NT)
    qd_gather.finish()
    fine_gather.across()

    k2 = two_heads(keys)
    v2 = two_heads(values)
    st_buf[...] = mm(k2, qd_all[:, :HD], NT)
    dpt_buf[...] = mm(v2, qd_all[:, HD:], NT)
    for step in range(1, peers):
        block = lax.rem(me - step + peers, peers)
        pltpu.make_async_remote_copy(
            src_ref=stats.at[block],
            dst_ref=stats.at[block],
            send_sem=stat_send.at[step],
            recv_sem=stat_recv.at[step],
            device_id={"tile": lower},
            device_id_type=pl.DeviceIdType.MESH,
        ).wait_recv()
    dk = jnp.zeros((2 * n, HD), jnp.float32)
    dv = jnp.zeros((2 * n, HD), jnp.float32)
    group = math.gcd(peers, 4)
    for at in range(0, peers, group):
        span = slice(at * n, (at + group) * n)

        def stat_rows(kind):
            heads = []
            for h in range(HEADS):
                parts = [stats[t, kind : kind + 1, h * n : (h + 1) * n] for t in range(at, at + group)]
                heads.append(jnp.broadcast_to(jnp.concatenate(parts, axis=1), (n, group * n)))
            return jnp.concatenate(heads, axis=0)

        prob_t = jnp.exp(st_buf[:, span] - stat_rows(0))
        dscore_t = (prob_t * (dpt_buf[:, span] - stat_rows(1))).astype(jnp.bfloat16)
        dv = dv + mm(prob_t.astype(jnp.bfloat16), qd_all[span, HD:])
        dk = dk + mm(dscore_t, qd_all[span, :HD])
    dkeys = pick_heads(dk).astype(jnp.bfloat16)
    dvalues = pick_heads(dv).astype(jnp.bfloat16)
    grad_h = grad_h + mm(dkeys, qk[1], NT) + mm(dvalues, vw[...], NT)
    dhidden = grad_h.astype(jnp.bfloat16)
    dh_all[mine, :] = dhidden
    dh_gather.own()

    def back_row(a, grads):
        even = mm(grads, conv[a, 1], NT)
        later = mm(grads, conv[a, 0], NT)
        later = jnp.where(row_at == n - 1, 0.0, pltpu.roll(later, n - 1, 0))
        return even, mm(grads, conv[a, 2], NT) + later

    even_mid, odd_mid = back_row(1, dhidden)
    grad_fine[0, :, :chans] = even_mid.astype(jnp.bfloat16)
    grad_fine[0, :, chans:] = odd_mid.astype(jnp.bfloat16)
    even_low, odd_low = back_row(2, dhidden)
    dh_gather.across()
    fine_gather.over()
    dh_gather.over()
    dh_gather.finish()
    below = dh_all[pl.ds(pl.multiple_of(lower * n, n), n), :]
    below = jnp.where(me == peers - 1, jnp.zeros_like(below), below)
    even_top, odd_top = back_row(0, below)
    grad_fine[1, :, :chans] = (even_low + even_top).astype(jnp.bfloat16)
    grad_fine[1, :, chans:] = (odd_low + odd_top).astype(jnp.bfloat16)
    for t in range(peers):
        span = slice(t * n, (t + 1) * n)
        moved = pltpu.roll(dh_all[span, :].astype(jnp.float32), n - 1, 0)
        shift_all[span, :] = jnp.where(row_at == n - 1, 0.0, moved).astype(jnp.bfloat16)
    fine_gather.finish()
    norm = 1.0 / math.sqrt(full)
    for a, row in ((1, 0), (2, 1), (0, 1)):
        for b in range(3):
            source = dh_all if b else shift_all
            at = row * 2 * chans + (0 if b == 1 else chans)
            features = slice(at, at + chans)
            if a == 0:
                part = mm(fine_t[features, : full - n], source[n:, :])
            else:
                part = mm(fine_t[features, :], source[...])
            grad_conv[3 * a + b] = part * norm
    halo.wait_send()
    for gather in (fine_gather, kv_gather, qd_gather, dh_gather):
        gather.drain()
    for made in stat_copies:
        made.wait_send()


def fused_body(fine, conv_weight, qk_weight, v_weight, o_weight, upstream):
    peers = lax.axis_size("tile")
    n, chans = upstream.shape
    full = n * peers
    pairs = fine.reshape(2, n, 2 * chans)
    vmem = pl.BlockSpec(memory_space=pltpu.VMEM)
    dma = pltpu.SemaphoreType.DMA
    block_out, grad_conv, grad_fine = pl.pallas_call(
        functools.partial(fused_kernel, peers),
        out_shape=(
            jax.ShapeDtypeStruct((n, chans), jnp.bfloat16),
            jax.ShapeDtypeStruct((9, chans, chans), jnp.float32),
            jax.ShapeDtypeStruct((2, n, 2 * chans), jnp.bfloat16),
        ),
        in_specs=[vmem] * 6,
        out_specs=(vmem, vmem, vmem),
        scratch_shapes=[
            pltpu.VMEM((n, 2 * chans), jnp.bfloat16),
            pltpu.VMEM((full, 2 * HD), jnp.bfloat16),
            pltpu.VMEM((full, 2 * HD), jnp.bfloat16),
            pltpu.VMEM((full, chans), jnp.bfloat16),
            pltpu.VMEM((full, chans), jnp.bfloat16),
            pltpu.VMEM((4 * chans, full), jnp.bfloat16),
            pltpu.VMEM((peers, 2, 2 * n), jnp.float32),
            pltpu.VMEM((2 * n, full), jnp.float32),
            pltpu.VMEM((2 * n, full), jnp.float32),
            dma((4, peers)),
            dma((4, peers)),
            dma((peers,)),
            dma((peers,)),
            dma,
            dma,
        ],
        compiler_params=pltpu.CompilerParams(
            collective_id=0, has_side_effects=True, vmem_limit_bytes=48 * 2**20
        ),
    )(pairs, conv_weight, qk_weight, v_weight, o_weight, upstream)
    return (
        block_out,
        grad_conv.reshape(3, 3, chans, chans),
        grad_fine.reshape(fine.shape),
    )


def solution(mesh):
    def whole(fine, *rest):
        devices = mesh.shape["groups"] * mesh.shape["tile"]
        one_row = fine.shape[0] == 2 * devices and fine.shape[1] == 256 and fine.shape[2] == 256
        fits = fine.size // mesh.shape["groups"] <= 4 * 2**20 and mesh.shape["tile"] % 4 == 0
        return jax.shard_map(
            fused_body if one_row and fits else body,
            mesh=mesh,
            in_specs=(
                P(("groups", "tile"), None, None),
                P(),
                P(),
                P(),
                P(),
                P(("groups", "tile"), None),
            ),
            out_specs=(
                P(("groups", "tile"), None),
                P("groups", None, None, None),
                P(("groups", "tile"), None, None),
            ),
            check_vma=False,
        )(fine, *rest)

    return whole
```

```python
import functools
import math

import jax
import jax.numpy as jnp
from jax import lax
from jax.experimental import pallas as pl
from jax.experimental.pallas import tpu as pltpu
from jax.sharding import PartitionSpec as P

HEADS = 2
HDIM = 64
HD = 128


def shifted(x, axis, by):
    peers = lax.axis_size(axis)
    pairs = [(i, i + by) for i in range(peers) if 0 <= i + by < peers]
    return lax.ppermute(x, axis, pairs)


def head_view(mat):
    return mat.reshape(mat.shape[0], HEADS, HDIM)


def score_block(queries, keys):
    product = jnp.einsum(
        "qhd,khd->hqk", head_view(queries), head_view(keys), preferred_element_type=jnp.float32
    )
    return product * HDIM ** (-0.5)


def dot_back(left, right):
    return lax.dot_general(
        left, right, (((1,), (1,)), ((), ())), preferred_element_type=jnp.float32
    )


def dot_over(left, right):
    return lax.dot_general(
        left, right, (((0,), (0,)), ((), ())), preferred_element_type=jnp.float32
    )


def body(fine, conv_weight, qk_weight, v_weight, o_weight, upstream):
    rows = fine.shape[0] // 2
    cols = fine.shape[1] // 2
    chans = fine.shape[2]
    local = rows * cols
    scale = HDIM ** (-0.5)
    above = shifted(fine[-1:], "tile", 1)
    padded = jnp.pad(jnp.concatenate([above, fine], axis=0), ((0, 0), (1, 0), (0, 0)))
    taps = []
    total = jnp.zeros((local, chans), jnp.float32)
    for a in range(3):
        for b in range(3):
            tap = padded[a : a + 2 * rows : 2, b : b + 2 * cols : 2].reshape(local, chans)
            taps.append(tap)
            total = total + jnp.dot(tap, conv_weight[a, b], preferred_element_type=jnp.float32)
    hidden = total.astype(jnp.bfloat16)
    query = jnp.dot(hidden, qk_weight[0], preferred_element_type=jnp.float32).astype(jnp.bfloat16)
    key_loc = jnp.dot(hidden, qk_weight[1], preferred_element_type=jnp.float32).astype(jnp.bfloat16)
    value_loc = jnp.dot(hidden, v_weight, preferred_element_type=jnp.float32).astype(jnp.bfloat16)
    keys_all, values_all = (
        lax.all_gather(key_loc, "tile", axis=0, tiled=True),
        lax.all_gather(value_loc, "tile", axis=0, tiled=True),
    )
    everyone = keys_all.shape[0]
    block = math.gcd(everyone, 2048)
    steps_total = everyone // block

    def stats_step(index, carry):
        top, summed = carry
        scores = score_block(query, lax.dynamic_slice_in_dim(keys_all, index * block, block, 0))
        new_top = jnp.maximum(top, jnp.max(scores, axis=2))
        summed = summed * jnp.exp(top - new_top) + jnp.sum(
            jnp.exp(scores - new_top[:, :, None]), axis=2
        )
        return (new_top, summed)

    start_top = jnp.full((HEADS, local), -jnp.inf, jnp.float32)
    top, summed = lax.fori_loop(
        0, steps_total, stats_step, (start_top, jnp.zeros((HEADS, local), jnp.float32))
    )
    lse = top + jnp.log(summed)

    def value_step(index, acc):
        scores = score_block(query, lax.dynamic_slice_in_dim(keys_all, index * block, block, 0))
        weights = jnp.exp(scores - lse[:, :, None]).astype(jnp.bfloat16)
        v_part = head_view(lax.dynamic_slice_in_dim(values_all, index * block, block, 0))
        return acc + jnp.einsum("hqk,khd->qhd", weights, v_part, preferred_element_type=jnp.float32)

    mixed = lax.fori_loop(0, steps_total, value_step, jnp.zeros((local, HEADS, HDIM), jnp.float32))
    attended = mixed.reshape(local, HD).astype(jnp.bfloat16)
    block_out = (
        hidden.astype(jnp.float32) + jnp.dot(attended, o_weight, preferred_element_type=jnp.float32)
    ).astype(jnp.bfloat16)
    dattended = dot_back(upstream, o_weight).astype(jnp.bfloat16)
    product = dattended.astype(jnp.float32) * attended.astype(jnp.float32)
    delta = jnp.sum(product.reshape(local, HEADS, HDIM), axis=2).T

    def query_step(index, acc):
        k_part = lax.dynamic_slice_in_dim(keys_all, index * block, block, 0)
        v_part = lax.dynamic_slice_in_dim(values_all, index * block, block, 0)
        prob = jnp.exp(score_block(query, k_part) - lse[:, :, None])
        dprob = jnp.einsum(
            "qhd,khd->hqk",
            head_view(dattended),
            head_view(v_part),
            preferred_element_type=jnp.float32,
        )
        dscore = (prob * (dprob - delta[:, :, None]) * scale).astype(jnp.bfloat16)
        return acc + jnp.einsum(
            "hqk,khd->qhd", dscore, head_view(k_part), preferred_element_type=jnp.float32
        )

    dq_acc = lax.fori_loop(0, steps_total, query_step, jnp.zeros((local, HEADS, HDIM), jnp.float32))
    dquery = dq_acc.reshape(local, HD).astype(jnp.bfloat16)
    lse_all, delta_all = (
        lax.all_gather(lse.T, "tile", axis=0, tiled=True),
        lax.all_gather(delta.T, "tile", axis=0, tiled=True),
    )
    empty = jnp.zeros((local, HEADS, HDIM), jnp.float32)
    q_in = lax.all_gather(query, "tile", axis=0, tiled=True)
    d_in = lax.all_gather(dattended, "tile", axis=0, tiled=True)
    incoming = q_in.shape[0]
    sub = math.gcd(incoming, 2048)

    def inner(index, acc):
        dk_acc, dv_acc = acc
        at = index * sub
        q_part = lax.dynamic_slice_in_dim(q_in, at, sub, 0)
        d_part = lax.dynamic_slice_in_dim(d_in, at, sub, 0)
        l_part = lax.dynamic_slice_in_dim(lse_all, at, sub, 0).T
        e_part = lax.dynamic_slice_in_dim(delta_all, at, sub, 0).T
        prob = jnp.exp(score_block(q_part, key_loc) - l_part[:, :, None])
        dv_acc = dv_acc + jnp.einsum(
            "hqk,qhd->khd",
            prob.astype(jnp.bfloat16),
            head_view(d_part),
            preferred_element_type=jnp.float32,
        )
        dprob = jnp.einsum(
            "qhd,khd->hqk",
            head_view(d_part),
            head_view(value_loc),
            preferred_element_type=jnp.float32,
        )
        dscore = (prob * (dprob - e_part[:, :, None]) * scale).astype(jnp.bfloat16)
        dk_acc = dk_acc + jnp.einsum(
            "hqk,qhd->khd", dscore, head_view(q_part), preferred_element_type=jnp.float32
        )
        return (dk_acc, dv_acc)

    dk_acc, dv_acc = lax.fori_loop(0, incoming // sub, inner, (empty, empty))
    dkeys = dk_acc.reshape(local, HD).astype(jnp.bfloat16)
    dvalues = dv_acc.reshape(local, HD).astype(jnp.bfloat16)
    dhidden = upstream.astype(jnp.float32)
    dhidden = dhidden + dot_back(dquery, qk_weight[0])
    dhidden = dhidden + dot_back(dkeys, qk_weight[1])
    dhidden = dhidden + dot_back(dvalues, v_weight)
    dhidden = dhidden.astype(jnp.bfloat16)
    kernel_rows = []
    dpadded = jnp.zeros((2 * rows + 1, 2 * cols + 1, chans), jnp.float32)
    for a in range(3):
        row_list = []
        for b in range(3):
            row_list.append(dot_over(taps[3 * a + b], dhidden))
            back = dot_back(dhidden, conv_weight[a, b])
            dpadded = dpadded.at[a : a + 2 * rows : 2, b : b + 2 * cols : 2].add(
                back.reshape(rows, cols, chans)
            )
        kernel_rows.append(jnp.stack(row_list))
    kernel_local = jnp.stack(kernel_rows)
    grad_conv = lax.psum(kernel_local, "tile") * (1.0 / math.sqrt(everyone))
    below = shifted(dpadded[0:1, 1:].astype(jnp.bfloat16), "tile", -1).astype(jnp.float32)
    grad_fine = dpadded[1:, 1:]
    grad_fine = grad_fine.at[-1:].add(below)
    return (block_out, grad_conv, grad_fine.astype(jnp.bfloat16))


NT = (((1,), (1,)), ((), ()))
NN = (((1,), (0,)), ((), ()))


def mm(left, right, dims=NN):
    return lax.dot_general(left, right, dims, preferred_element_type=jnp.float32)


def two_heads(mat):
    lane = lax.broadcasted_iota(jnp.int32, mat.shape, 1)
    zero = jnp.zeros_like(mat)
    return jnp.concatenate(
        [jnp.where(lane < HDIM, mat, zero), jnp.where(lane < HDIM, zero, mat)], axis=0
    )


def pick_heads(mat):
    half = mat.shape[0] // 2
    lane = lax.broadcasted_iota(jnp.int32, (half, mat.shape[1]), 1)
    return jnp.where(lane < HDIM, mat[:half], mat[half:])


class Gather:
    def __init__(self, view, me, peers, send, recv, slot):
        self.view, self.peers, self.send, self.recv, self.slot = view, peers, send, recv, slot
        self.zs = peers // 4
        self.core = lax.rem(me, 2)
        self.x = lax.rem(lax.div(me, 2), 2)
        self.z = lax.div(me, 4)
        self.me = me
        self.copies = []

    def at(self, dz, flip_x=0, flip_core=0):
        z = lax.rem(self.z + dz + self.zs, self.zs)
        x = 1 - self.x if flip_x else self.x
        core = 1 - self.core if flip_core else self.core
        return z * 4 + x * 2 + core

    def copy(self, index, block, target):
        return pltpu.make_async_remote_copy(
            src_ref=self.view(block),
            dst_ref=self.view(block),
            send_sem=self.send.at[self.slot, index],
            recv_sem=self.recv.at[self.slot, index],
            device_id={"tile": target},
            device_id_type=pl.DeviceIdType.MESH,
        )

    def go(self, index, block, target):
        made = self.copy(index, block, target)
        made.start()
        self.copies.append(made)

    def landed(self, index, block):
        self.copy(index, block, self.at(0, 1)).wait_recv()

    def own(self):
        zs = self.zs
        for d in range(1, zs):
            self.go(d - 1, self.me, self.at(d))
        self.go(zs - 1, self.me, self.at(0, 1))
        self.go(2 * zs - 1, self.me, self.at(0, 0, 1))

    def across(self):
        zs = self.zs
        for d in range(1, zs):
            block = self.at(-d)
            self.landed(d - 1, block)
            self.go(zs - 1 + d, block, self.at(0, 1))
            self.go(2 * zs - 1 + d, block, self.at(0, 0, 1))

    def over(self):
        zs = self.zs
        for d in range(zs):
            block = self.at(-d, 1)
            self.landed(zs - 1 + d, block)
            self.go(3 * zs - 1 + d, block, self.at(0, 0, 1))

    def finish(self):
        zs = self.zs
        for d in range(zs):
            self.landed(2 * zs - 1 + d, self.at(-d, 0, 1))
            self.landed(3 * zs - 1 + d, self.at(-d, 1, 1))

    def drain(self):
        for made in self.copies:
            made.wait_send()


def fused_kernel(
    peers,
    fine_hbm,
    conv_hbm,
    qk_hbm,
    vw_hbm,
    ow_hbm,
    up_hbm,
    block_hbm,
    grad_conv_hbm,
    grad_fine_hbm,
    fine,
    conv,
    qk,
    vw,
    ow,
    up,
    block_out,
    grad_conv,
    grad_fine,
    in_sem,
    out_sem,
    above,
    hid_all,
    kv_all,
    q_all,
    d_all,
    dh_all,
    shift_all,
    fine_t,
    stats,
    st_buf,
    dpt_buf,
    send,
    recv,
    stat_send,
    stat_recv,
    halo_send,
    halo_recv,
):
    me = lax.axis_index("tile")
    n = up.shape[0]
    chans = up.shape[1]
    full = n * peers
    lower = lax.rem(me + 1, peers)
    moves = (
        (fine_hbm, fine), (up_hbm, up), (ow_hbm, ow), (conv_hbm, conv), (qk_hbm, qk), (vw_hbm, vw)
    )
    loads = [pltpu.make_async_copy(a, b, in_sem.at[i]) for i, (a, b) in enumerate(moves)]
    for load in loads:
        load.start()
    stores = []

    def store(source, target):
        made = pltpu.make_async_copy(source, target, out_sem.at[len(stores)])
        made.start()
        stores.append(made)

    barrier = pltpu.get_barrier_semaphore()
    for step in range(1, peers):
        pl.semaphore_signal(
            barrier,
            inc=1,
            device_id={"tile": lax.rem(me + step, peers)},
            device_id_type=pl.DeviceIdType.MESH,
        )

    def rows(ref):
        return lambda t: ref.at[pl.ds(pl.multiple_of(t * n, n), n), :]

    def cols(ref, part):
        lines = pl.ds(part * chans, chans)
        return lambda t: ref.at[lines, pl.ds(pl.multiple_of(t * n, n), n)]

    mine = pl.ds(pl.multiple_of(me * n, n), n)
    loads[0].wait()
    pl.semaphore_wait(barrier, peers - 1)
    halo = pltpu.make_async_remote_copy(
        src_ref=fine.at[1],
        dst_ref=above,
        send_sem=halo_send,
        recv_sem=halo_recv,
        device_id={"tile": lower},
        device_id_type=pl.DeviceIdType.MESH,
    )
    halo.start()
    fine_t[: 2 * chans, mine] = fine[0].T
    parts = [Gather(cols(fine_t, p), me, peers, send, recv, i) for i, p in enumerate((0, 1, 3, 2))]
    hid_gather = Gather(rows(hid_all), me, peers, send, recv, 4)
    d_gather = Gather(rows(d_all), me, peers, send, recv, 5)
    dh_gather = Gather(rows(dh_all), me, peers, send, recv, 6)
    parts[0].own()
    for load in loads[1:]:
        load.wait()

    def conv_row(a, row):
        straight = mm(row[:, :chans], conv[a, 1]) + mm(row[:, chans:], conv[a, 2])
        return straight, mm(row[:, chans:], conv[a, 0])

    mid, mid_late = conv_row(1, fine[0])
    low, low_late = conv_row(2, fine[1])
    dattended = mm(up[...], ow[...], NT).astype(jnp.bfloat16)
    fine_t[2 * chans :, mine] = fine[1].T
    halo.wait_recv()
    top_row = jnp.where(me == 0, jnp.zeros_like(above[...]), above[...])
    top, top_late = conv_row(0, top_row)
    late = top_late + mid_late + low_late
    row_at = lax.broadcasted_iota(jnp.int32, (n, chans), 0)
    late = jnp.where(row_at == 0, 0.0, pltpu.roll(late, 1, 0))
    hidden = (top + mid + low + late).astype(jnp.bfloat16)
    hid_all[mine, :] = hidden
    hid_gather.own()
    d_all[mine, :] = dattended
    keys = mm(hidden, qk[1]).astype(jnp.bfloat16)
    values = mm(hidden, vw[...]).astype(jnp.bfloat16)

    def scaled_query(mat):
        full_query = mm(mat, qk[0]).astype(jnp.bfloat16)
        return (full_query.astype(jnp.float32) * HDIM**-0.5).astype(jnp.bfloat16)

    query = scaled_query(hidden)
    q2 = two_heads(query)
    d2 = two_heads(dattended)
    parts[0].across()
    hid_gather.across()
    d_gather.own()
    parts[1].own()
    hid_gather.over()
    parts[0].over()
    hid_gather.finish()
    kv_all[:, :HD] = mm(hid_all[...], qk[1]).astype(jnp.bfloat16)
    kv_all[:, HD:] = mm(hid_all[...], vw[...]).astype(jnp.bfloat16)
    scores = mm(q2, kv_all[:, :HD], NT)
    high = jnp.max(scores, axis=1, keepdims=True)
    expd = jnp.exp(scores - high)
    total = jnp.sum(expd, axis=1, keepdims=True)
    lse = high + jnp.log(total)
    prob = expd * (1.0 / total)
    attended = pick_heads(mm(prob.astype(jnp.bfloat16), kv_all[:, HD:])).astype(jnp.bfloat16)
    product = dattended.astype(jnp.float32) * attended.astype(jnp.float32)
    delta = jnp.sum(two_heads(product), axis=1, keepdims=True)
    lane = lax.broadcasted_iota(jnp.int32, (2 * n, 128), 1)
    packed = jnp.where(lane == 0, lse, jnp.where(lane == 1, delta, 0.0)).T
    stats[me] = packed[:2]
    stat_copies = []
    for step in range(1, peers):
        made = pltpu.make_async_remote_copy(
            src_ref=stats.at[me],
            dst_ref=stats.at[me],
            send_sem=stat_send.at[step],
            recv_sem=stat_recv.at[step],
            device_id={"tile": lax.rem(me + step, peers)},
            device_id_type=pl.DeviceIdType.MESH,
        )
        made.start()
        stat_copies.append(made)
    d_gather.across()
    block_out[...] = (hidden.astype(jnp.float32) + mm(attended, ow[...])).astype(jnp.bfloat16)
    store(block_out, block_hbm)
    q_all[...] = scaled_query(hid_all[...])
    d_gather.over()
    parts[1].across()
    parts[2].own()
    dprob = mm(d2, kv_all[:, HD:], NT)
    dscore = (prob * (dprob - delta)).astype(jnp.bfloat16)
    dquery = (pick_heads(mm(dscore, kv_all[:, :HD])) * HDIM**-0.5).astype(jnp.bfloat16)
    grad_h = up[...].astype(jnp.float32) + mm(dquery, qk[0], NT)
    d_gather.finish()

    k2 = two_heads(keys)
    v2 = two_heads(values)
    st_buf[...] = mm(k2, q_all[...], NT)
    dpt_buf[...] = mm(v2, d_all[...], NT)
    for step in range(1, peers):
        block = lax.rem(me - step + peers, peers)
        pltpu.make_async_remote_copy(
            src_ref=stats.at[block],
            dst_ref=stats.at[block],
            send_sem=stat_send.at[step],
            recv_sem=stat_recv.at[step],
            device_id={"tile": lower},
            device_id_type=pl.DeviceIdType.MESH,
        ).wait_recv()
    dk = jnp.zeros((2 * n, HD), jnp.float32)
    dv = jnp.zeros((2 * n, HD), jnp.float32)
    group = math.gcd(peers, 4)
    for at in range(0, peers, group):
        span = slice(at * n, (at + group) * n)

        def stat_rows(kind):
            heads = []
            for h in range(HEADS):
                parts = [stats[t, kind : kind + 1, h * n : (h + 1) * n] for t in range(at, at + group)]
                heads.append(jnp.broadcast_to(jnp.concatenate(parts, axis=1), (n, group * n)))
            return jnp.concatenate(heads, axis=0)

        prob_t = jnp.exp(st_buf[:, span] - stat_rows(0))
        dscore_t = (prob_t * (dpt_buf[:, span] - stat_rows(1))).astype(jnp.bfloat16)
        dv = dv + mm(prob_t.astype(jnp.bfloat16), d_all[span, :])
        dk = dk + mm(dscore_t, q_all[span, :])
    dkeys = pick_heads(dk).astype(jnp.bfloat16)
    dvalues = pick_heads(dv).astype(jnp.bfloat16)
    grad_h = grad_h + mm(dkeys, qk[1], NT) + mm(dvalues, vw[...], NT)
    dhidden = grad_h.astype(jnp.bfloat16)
    dh_all[mine, :] = dhidden
    dh_gather.own()
    parts[1].over()
    parts[2].across()
    parts[3].own()

    def back_row(a, grads):
        even = mm(grads, conv[a, 1], NT)
        later = mm(grads, conv[a, 0], NT)
        later = jnp.where(row_at == n - 1, 0.0, pltpu.roll(later, n - 1, 0))
        return even, mm(grads, conv[a, 2], NT) + later

    even_mid, odd_mid = back_row(1, dhidden)
    grad_fine[0, :, :chans] = even_mid.astype(jnp.bfloat16)
    grad_fine[0, :, chans:] = odd_mid.astype(jnp.bfloat16)
    even_low, odd_low = back_row(2, dhidden)
    dh_gather.across()
    dh_gather.over()
    parts[2].over()
    parts[3].across()
    dh_gather.finish()
    below = dh_all[pl.ds(pl.multiple_of(lower * n, n), n), :]
    below = jnp.where(me == peers - 1, jnp.zeros_like(below), below)
    even_top, odd_top = back_row(0, below)
    grad_fine[1, :, :chans] = (even_low + even_top).astype(jnp.bfloat16)
    grad_fine[1, :, chans:] = (odd_low + odd_top).astype(jnp.bfloat16)
    for t in range(peers):
        span = slice(t * n, (t + 1) * n)
        moved = pltpu.roll(dh_all[span, :].astype(jnp.float32), n - 1, 0)
        shift_all[span, :] = jnp.where(row_at == n - 1, 0.0, moved).astype(jnp.bfloat16)
    store(grad_fine, grad_fine_hbm)
    norm = 1.0 / math.sqrt(full)

    def finish_tap(a, b):
        source = dh_all if b else shift_all
        at = (2 if a != 1 else 0) * chans + (0 if b == 1 else chans)
        features = slice(at, at + chans)
        if a == 0:
            part = mm(fine_t[features, : full - n], source[n:, :])
        else:
            part = mm(fine_t[features, :], source[...])
        grad_conv[3 * a + b] = part * norm
        store(grad_conv.at[3 * a + b], grad_conv_hbm.at[3 * a + b])

    parts[0].finish()
    finish_tap(1, 1)
    parts[1].finish()
    finish_tap(1, 2)
    parts[3].over()
    finish_tap(1, 0)
    parts[2].finish()
    for a in (2, 0):
        for b in (2, 0):
            finish_tap(a, b)
    parts[3].finish()
    for a in (2, 0):
        finish_tap(a, 1)
    halo.wait_send()
    for gather in (*parts, hid_gather, d_gather, dh_gather):
        gather.drain()
    for made in stat_copies:
        made.wait_send()
    for made in stores:
        made.wait()


def fused_body(fine, conv_weight, qk_weight, v_weight, o_weight, upstream):
    peers = lax.axis_size("tile")
    n, chans = upstream.shape
    full = n * peers
    pairs = fine.reshape(2, n, 2 * chans)
    hbm = pl.BlockSpec(memory_space=pl.ANY)
    dma = pltpu.SemaphoreType.DMA
    block_out, grad_conv, grad_fine = pl.pallas_call(
        functools.partial(fused_kernel, peers),
        out_shape=(
            jax.ShapeDtypeStruct((n, chans), jnp.bfloat16),
            jax.ShapeDtypeStruct((9, chans, chans), jnp.float32),
            jax.ShapeDtypeStruct((2, n, 2 * chans), jnp.bfloat16),
        ),
        in_specs=[hbm] * 6,
        out_specs=(hbm, hbm, hbm),
        scratch_shapes=[
            pltpu.VMEM(pairs.shape, jnp.bfloat16),
            pltpu.VMEM(conv_weight.shape, jnp.bfloat16),
            pltpu.VMEM(qk_weight.shape, jnp.bfloat16),
            pltpu.VMEM(v_weight.shape, jnp.bfloat16),
            pltpu.VMEM(o_weight.shape, jnp.bfloat16),
            pltpu.VMEM(upstream.shape, jnp.bfloat16),
            pltpu.VMEM((n, chans), jnp.bfloat16),
            pltpu.VMEM((9, chans, chans), jnp.float32),
            pltpu.VMEM((2, n, 2 * chans), jnp.bfloat16),
            dma((6,)),
            dma((11,)),
            pltpu.VMEM((n, 2 * chans), jnp.bfloat16),
            pltpu.VMEM((full, chans), jnp.bfloat16),
            pltpu.VMEM((full, 2 * HD), jnp.bfloat16),
            pltpu.VMEM((full, HD), jnp.bfloat16),
            pltpu.VMEM((full, HD), jnp.bfloat16),
            pltpu.VMEM((full, chans), jnp.bfloat16),
            pltpu.VMEM((full, chans), jnp.bfloat16),
            pltpu.VMEM((4 * chans, full), jnp.bfloat16),
            pltpu.VMEM((peers, 2, 2 * n), jnp.float32),
            pltpu.VMEM((2 * n, full), jnp.float32),
            pltpu.VMEM((2 * n, full), jnp.float32),
            dma((7, peers)),
            dma((7, peers)),
            dma((peers,)),
            dma((peers,)),
            dma,
            dma,
        ],
        compiler_params=pltpu.CompilerParams(
            collective_id=0, has_side_effects=True, vmem_limit_bytes=60 * 2**20
        ),
    )(pairs, conv_weight, qk_weight, v_weight, o_weight, upstream)
    return (
        block_out,
        grad_conv.reshape(3, 3, chans, chans),
        grad_fine.reshape(fine.shape),
    )


def solution(mesh):
    def whole(fine, *rest):
        devices = mesh.shape["groups"] * mesh.shape["tile"]
        one_row = fine.shape[0] == 2 * devices and fine.shape[1] == 256 and fine.shape[2] == 256
        fits = fine.size // mesh.shape["groups"] <= 4 * 2**20 and mesh.shape["tile"] % 4 == 0
        return jax.shard_map(
            fused_body if one_row and fits else body,
            mesh=mesh,
            in_specs=(
                P(("groups", "tile"), None, None),
                P(),
                P(),
                P(),
                P(),
                P(("groups", "tile"), None),
            ),
            out_specs=(
                P(("groups", "tile"), None),
                P("groups", None, None, None),
                P(("groups", "tile"), None, None),
            ),
            check_vma=False,
        )(fine, *rest)

    return whole
```

```python
import functools
import math

import jax
import jax.numpy as jnp
from jax import lax
from jax.experimental import pallas as pl
from jax.experimental.pallas import tpu as pltpu
from jax.sharding import PartitionSpec as P

HEADS = 2
HDIM = 64
HD = 128


def shifted(x, axis, by):
    peers = lax.axis_size(axis)
    pairs = [(i, i + by) for i in range(peers) if 0 <= i + by < peers]
    return lax.ppermute(x, axis, pairs)


def head_view(mat):
    return mat.reshape(mat.shape[0], HEADS, HDIM)


def score_block(queries, keys):
    product = jnp.einsum(
        "qhd,khd->hqk", head_view(queries), head_view(keys), preferred_element_type=jnp.float32
    )
    return product * HDIM ** (-0.5)


def dot_back(left, right):
    return lax.dot_general(
        left, right, (((1,), (1,)), ((), ())), preferred_element_type=jnp.float32
    )


def dot_over(left, right):
    return lax.dot_general(
        left, right, (((0,), (0,)), ((), ())), preferred_element_type=jnp.float32
    )


def body(fine, conv_weight, qk_weight, v_weight, o_weight, upstream):
    rows = fine.shape[0] // 2
    cols = fine.shape[1] // 2
    chans = fine.shape[2]
    local = rows * cols
    scale = HDIM ** (-0.5)
    above = shifted(fine[-1:], "tile", 1)
    padded = jnp.pad(jnp.concatenate([above, fine], axis=0), ((0, 0), (1, 0), (0, 0)))
    taps = []
    total = jnp.zeros((local, chans), jnp.float32)
    for a in range(3):
        for b in range(3):
            tap = padded[a : a + 2 * rows : 2, b : b + 2 * cols : 2].reshape(local, chans)
            taps.append(tap)
            total = total + jnp.dot(tap, conv_weight[a, b], preferred_element_type=jnp.float32)
    hidden = total.astype(jnp.bfloat16)
    query = jnp.dot(hidden, qk_weight[0], preferred_element_type=jnp.float32).astype(jnp.bfloat16)
    key_loc = jnp.dot(hidden, qk_weight[1], preferred_element_type=jnp.float32).astype(jnp.bfloat16)
    value_loc = jnp.dot(hidden, v_weight, preferred_element_type=jnp.float32).astype(jnp.bfloat16)
    keys_all, values_all = (
        lax.all_gather(key_loc, "tile", axis=0, tiled=True),
        lax.all_gather(value_loc, "tile", axis=0, tiled=True),
    )
    everyone = keys_all.shape[0]
    block = math.gcd(everyone, 2048)
    steps_total = everyone // block

    def stats_step(index, carry):
        top, summed = carry
        scores = score_block(query, lax.dynamic_slice_in_dim(keys_all, index * block, block, 0))
        new_top = jnp.maximum(top, jnp.max(scores, axis=2))
        summed = summed * jnp.exp(top - new_top) + jnp.sum(
            jnp.exp(scores - new_top[:, :, None]), axis=2
        )
        return (new_top, summed)

    start_top = jnp.full((HEADS, local), -jnp.inf, jnp.float32)
    top, summed = lax.fori_loop(
        0, steps_total, stats_step, (start_top, jnp.zeros((HEADS, local), jnp.float32))
    )
    lse = top + jnp.log(summed)

    def value_step(index, acc):
        scores = score_block(query, lax.dynamic_slice_in_dim(keys_all, index * block, block, 0))
        weights = jnp.exp(scores - lse[:, :, None]).astype(jnp.bfloat16)
        v_part = head_view(lax.dynamic_slice_in_dim(values_all, index * block, block, 0))
        return acc + jnp.einsum("hqk,khd->qhd", weights, v_part, preferred_element_type=jnp.float32)

    mixed = lax.fori_loop(0, steps_total, value_step, jnp.zeros((local, HEADS, HDIM), jnp.float32))
    attended = mixed.reshape(local, HD).astype(jnp.bfloat16)
    block_out = (
        hidden.astype(jnp.float32) + jnp.dot(attended, o_weight, preferred_element_type=jnp.float32)
    ).astype(jnp.bfloat16)
    dattended = dot_back(upstream, o_weight).astype(jnp.bfloat16)
    product = dattended.astype(jnp.float32) * attended.astype(jnp.float32)
    delta = jnp.sum(product.reshape(local, HEADS, HDIM), axis=2).T

    def query_step(index, acc):
        k_part = lax.dynamic_slice_in_dim(keys_all, index * block, block, 0)
        v_part = lax.dynamic_slice_in_dim(values_all, index * block, block, 0)
        prob = jnp.exp(score_block(query, k_part) - lse[:, :, None])
        dprob = jnp.einsum(
            "qhd,khd->hqk",
            head_view(dattended),
            head_view(v_part),
            preferred_element_type=jnp.float32,
        )
        dscore = (prob * (dprob - delta[:, :, None]) * scale).astype(jnp.bfloat16)
        return acc + jnp.einsum(
            "hqk,khd->qhd", dscore, head_view(k_part), preferred_element_type=jnp.float32
        )

    dq_acc = lax.fori_loop(0, steps_total, query_step, jnp.zeros((local, HEADS, HDIM), jnp.float32))
    dquery = dq_acc.reshape(local, HD).astype(jnp.bfloat16)
    lse_all, delta_all = (
        lax.all_gather(lse.T, "tile", axis=0, tiled=True),
        lax.all_gather(delta.T, "tile", axis=0, tiled=True),
    )
    empty = jnp.zeros((local, HEADS, HDIM), jnp.float32)
    q_in = lax.all_gather(query, "tile", axis=0, tiled=True)
    d_in = lax.all_gather(dattended, "tile", axis=0, tiled=True)
    incoming = q_in.shape[0]
    sub = math.gcd(incoming, 2048)

    def inner(index, acc):
        dk_acc, dv_acc = acc
        at = index * sub
        q_part = lax.dynamic_slice_in_dim(q_in, at, sub, 0)
        d_part = lax.dynamic_slice_in_dim(d_in, at, sub, 0)
        l_part = lax.dynamic_slice_in_dim(lse_all, at, sub, 0).T
        e_part = lax.dynamic_slice_in_dim(delta_all, at, sub, 0).T
        prob = jnp.exp(score_block(q_part, key_loc) - l_part[:, :, None])
        dv_acc = dv_acc + jnp.einsum(
            "hqk,qhd->khd",
            prob.astype(jnp.bfloat16),
            head_view(d_part),
            preferred_element_type=jnp.float32,
        )
        dprob = jnp.einsum(
            "qhd,khd->hqk",
            head_view(d_part),
            head_view(value_loc),
            preferred_element_type=jnp.float32,
        )
        dscore = (prob * (dprob - e_part[:, :, None]) * scale).astype(jnp.bfloat16)
        dk_acc = dk_acc + jnp.einsum(
            "hqk,qhd->khd", dscore, head_view(q_part), preferred_element_type=jnp.float32
        )
        return (dk_acc, dv_acc)

    dk_acc, dv_acc = lax.fori_loop(0, incoming // sub, inner, (empty, empty))
    dkeys = dk_acc.reshape(local, HD).astype(jnp.bfloat16)
    dvalues = dv_acc.reshape(local, HD).astype(jnp.bfloat16)
    dhidden = upstream.astype(jnp.float32)
    dhidden = dhidden + dot_back(dquery, qk_weight[0])
    dhidden = dhidden + dot_back(dkeys, qk_weight[1])
    dhidden = dhidden + dot_back(dvalues, v_weight)
    dhidden = dhidden.astype(jnp.bfloat16)
    kernel_rows = []
    dpadded = jnp.zeros((2 * rows + 1, 2 * cols + 1, chans), jnp.float32)
    for a in range(3):
        row_list = []
        for b in range(3):
            row_list.append(dot_over(taps[3 * a + b], dhidden))
            back = dot_back(dhidden, conv_weight[a, b])
            dpadded = dpadded.at[a : a + 2 * rows : 2, b : b + 2 * cols : 2].add(
                back.reshape(rows, cols, chans)
            )
        kernel_rows.append(jnp.stack(row_list))
    kernel_local = jnp.stack(kernel_rows)
    grad_conv = lax.psum(kernel_local, "tile") * (1.0 / math.sqrt(everyone))
    below = shifted(dpadded[0:1, 1:].astype(jnp.bfloat16), "tile", -1).astype(jnp.float32)
    grad_fine = dpadded[1:, 1:]
    grad_fine = grad_fine.at[-1:].add(below)
    return (block_out, grad_conv, grad_fine.astype(jnp.bfloat16))


NT = (((1,), (1,)), ((), ()))
NN = (((1,), (0,)), ((), ()))


def mm(left, right, dims=NN):
    return lax.dot_general(left, right, dims, preferred_element_type=jnp.float32)


def two_heads(mat):
    lane = lax.broadcasted_iota(jnp.int32, mat.shape, 1)
    zero = jnp.zeros_like(mat)
    return jnp.concatenate(
        [jnp.where(lane < HDIM, mat, zero), jnp.where(lane < HDIM, zero, mat)], axis=0
    )


def pick_heads(mat):
    half = mat.shape[0] // 2
    lane = lax.broadcasted_iota(jnp.int32, (half, mat.shape[1]), 1)
    return jnp.where(lane < HDIM, mat[:half], mat[half:])


class Gather:
    def __init__(self, view, me, peers, send, recv, slot):
        self.view, self.peers, self.send, self.recv, self.slot = view, peers, send, recv, slot
        self.zs = peers // 4
        self.core = lax.rem(me, 2)
        self.x = lax.rem(lax.div(me, 2), 2)
        self.z = lax.div(me, 4)
        self.me = me
        self.copies = []

    def at(self, dz, flip_x=0, flip_core=0):
        z = lax.rem(self.z + dz + self.zs, self.zs)
        x = 1 - self.x if flip_x else self.x
        core = 1 - self.core if flip_core else self.core
        return z * 4 + x * 2 + core

    def copy(self, index, block, target):
        return pltpu.make_async_remote_copy(
            src_ref=self.view(block),
            dst_ref=self.view(block),
            send_sem=self.send.at[self.slot, index],
            recv_sem=self.recv.at[self.slot, index],
            device_id={"tile": target},
            device_id_type=pl.DeviceIdType.MESH,
        )

    def go(self, index, block, target):
        made = self.copy(index, block, target)
        made.start()
        self.copies.append(made)

    def landed(self, index, block):
        self.copy(index, block, self.at(0, 1)).wait_recv()

    def own(self):
        zs = self.zs
        for d in range(1, zs):
            self.go(d - 1, self.me, self.at(d))
        self.go(zs - 1, self.me, self.at(0, 1))
        self.go(2 * zs - 1, self.me, self.at(0, 0, 1))

    def across(self):
        zs = self.zs
        for d in range(1, zs):
            block = self.at(-d)
            self.landed(d - 1, block)
            self.go(zs - 1 + d, block, self.at(0, 1))
            self.go(2 * zs - 1 + d, block, self.at(0, 0, 1))

    def over(self):
        zs = self.zs
        for d in range(zs):
            block = self.at(-d, 1)
            self.landed(zs - 1 + d, block)
            self.go(3 * zs - 1 + d, block, self.at(0, 0, 1))

    def finish(self):
        zs = self.zs
        for d in range(zs):
            self.landed(2 * zs - 1 + d, self.at(-d, 0, 1))
            self.landed(3 * zs - 1 + d, self.at(-d, 1, 1))

    def drain(self):
        for made in self.copies:
            made.wait_send()


def fused_kernel(
    peers,
    fine_hbm,
    conv_hbm,
    qk_hbm,
    vw_hbm,
    ow_hbm,
    up_hbm,
    block_hbm,
    grad_conv_hbm,
    grad_fine_hbm,
    fine,
    conv,
    qk,
    vw,
    ow,
    up,
    block_out,
    grad_conv,
    grad_fine,
    in_sem,
    out_sem,
    above,
    hid_all,
    kv_all,
    q_all,
    d_all,
    dh_all,
    shift_all,
    fine_t,
    stats,
    st_buf,
    dpt_buf,
    send,
    recv,
    stat_send,
    stat_recv,
    halo_send,
    halo_recv,
):
    me = lax.axis_index("tile")
    n = up.shape[0]
    chans = up.shape[1]
    full = n * peers
    lower = lax.rem(me + 1, peers)
    moves = (
        (fine_hbm, fine), (up_hbm, up), (ow_hbm, ow), (conv_hbm, conv), (qk_hbm, qk), (vw_hbm, vw)
    )
    loads = [pltpu.make_async_copy(a, b, in_sem.at[i]) for i, (a, b) in enumerate(moves)]
    for load in loads:
        load.start()
    stores = []

    def store(source, target):
        made = pltpu.make_async_copy(source, target, out_sem.at[len(stores)])
        made.start()
        stores.append(made)

    barrier = pltpu.get_barrier_semaphore()
    for step in range(1, peers):
        pl.semaphore_signal(
            barrier,
            inc=1,
            device_id={"tile": lax.rem(me + step, peers)},
            device_id_type=pl.DeviceIdType.MESH,
        )

    def rows(ref):
        return lambda t: ref.at[pl.ds(pl.multiple_of(t * n, n), n), :]

    def cols(ref, part):
        lines = pl.ds(part * chans, chans)
        return lambda t: ref.at[t, lines, :]

    mine = pl.ds(pl.multiple_of(me * n, n), n)
    loads[0].wait()
    pl.semaphore_wait(barrier, peers - 1)
    halo = pltpu.make_async_remote_copy(
        src_ref=fine.at[1],
        dst_ref=above,
        send_sem=halo_send,
        recv_sem=halo_recv,
        device_id={"tile": lower},
        device_id_type=pl.DeviceIdType.MESH,
    )
    halo.start()
    fine_t[me, : 2 * chans, :] = fine[0].T
    parts = [Gather(cols(fine_t, p), me, peers, send, recv, i) for i, p in enumerate((0, 1, 3, 2))]
    hid_gather = Gather(rows(hid_all), me, peers, send, recv, 4)
    d_gather = Gather(rows(d_all), me, peers, send, recv, 5)
    dh_gather = Gather(rows(dh_all), me, peers, send, recv, 6)
    parts[0].own()
    for load in loads[1:]:
        load.wait()

    def conv_row(a, row):
        straight = mm(row[:, :chans], conv[a, 1]) + mm(row[:, chans:], conv[a, 2])
        return straight, mm(row[:, chans:], conv[a, 0])

    mid, mid_late = conv_row(1, fine[0])
    low, low_late = conv_row(2, fine[1])
    dattended = mm(up[...], ow[...], NT).astype(jnp.bfloat16)
    fine_t[me, 2 * chans :, :] = fine[1].T
    halo.wait_recv()
    top_row = jnp.where(me == 0, jnp.zeros_like(above[...]), above[...])
    top, top_late = conv_row(0, top_row)
    late = top_late + mid_late + low_late
    row_at = lax.broadcasted_iota(jnp.int32, (n, chans), 0)
    late = jnp.where(row_at == 0, 0.0, pltpu.roll(late, 1, 0))
    hidden = (top + mid + low + late).astype(jnp.bfloat16)
    hid_all[mine, :] = hidden
    hid_gather.own()
    d_all[mine, :] = dattended
    keys = mm(hidden, qk[1]).astype(jnp.bfloat16)
    values = mm(hidden, vw[...]).astype(jnp.bfloat16)

    def scaled_query(mat):
        full_query = mm(mat, qk[0]).astype(jnp.bfloat16)
        return (full_query.astype(jnp.float32) * HDIM**-0.5).astype(jnp.bfloat16)

    query = scaled_query(hidden)
    q2 = two_heads(query)
    d2 = two_heads(dattended)
    parts[0].across()
    hid_gather.across()
    d_gather.own()
    parts[1].own()
    hid_gather.over()
    parts[0].over()
    hid_gather.finish()
    kv_all[:, :HD] = mm(hid_all[...], qk[1]).astype(jnp.bfloat16)
    kv_all[:, HD:] = mm(hid_all[...], vw[...]).astype(jnp.bfloat16)
    scores = mm(q2, kv_all[:, :HD], NT)
    high = jnp.max(scores, axis=1, keepdims=True)
    expd = jnp.exp(scores - high)
    total = jnp.sum(expd, axis=1, keepdims=True)
    lse = high + jnp.log(total)
    prob = expd * (1.0 / total)
    attended = pick_heads(mm(prob.astype(jnp.bfloat16), kv_all[:, HD:])).astype(jnp.bfloat16)
    product = dattended.astype(jnp.float32) * attended.astype(jnp.float32)
    delta = jnp.sum(two_heads(product), axis=1, keepdims=True)
    lane = lax.broadcasted_iota(jnp.int32, (2 * n, 128), 1)
    packed = jnp.where(lane == 0, lse, jnp.where(lane == 1, delta, 0.0)).T
    stats[me] = packed[:2]
    stat_copies = []
    for step in range(1, peers):
        made = pltpu.make_async_remote_copy(
            src_ref=stats.at[me],
            dst_ref=stats.at[me],
            send_sem=stat_send.at[step],
            recv_sem=stat_recv.at[step],
            device_id={"tile": lax.rem(me + step, peers)},
            device_id_type=pl.DeviceIdType.MESH,
        )
        made.start()
        stat_copies.append(made)
    d_gather.across()
    block_out[...] = (hidden.astype(jnp.float32) + mm(attended, ow[...])).astype(jnp.bfloat16)
    store(block_out, block_hbm)
    q_all[...] = scaled_query(hid_all[...])
    d_gather.over()
    parts[1].across()
    parts[2].own()
    dprob = mm(d2, kv_all[:, HD:], NT)
    dscore = (prob * (dprob - delta)).astype(jnp.bfloat16)
    dquery = (pick_heads(mm(dscore, kv_all[:, :HD])) * HDIM**-0.5).astype(jnp.bfloat16)
    grad_h = up[...].astype(jnp.float32) + mm(dquery, qk[0], NT)
    d_gather.finish()

    k2 = two_heads(keys)
    v2 = two_heads(values)
    st_buf[...] = mm(k2, q_all[...], NT)
    dpt_buf[...] = mm(v2, d_all[...], NT)
    for step in range(1, peers):
        block = lax.rem(me - step + peers, peers)
        pltpu.make_async_remote_copy(
            src_ref=stats.at[block],
            dst_ref=stats.at[block],
            send_sem=stat_send.at[step],
            recv_sem=stat_recv.at[step],
            device_id={"tile": lower},
            device_id_type=pl.DeviceIdType.MESH,
        ).wait_recv()
    dk = jnp.zeros((2 * n, HD), jnp.float32)
    dv = jnp.zeros((2 * n, HD), jnp.float32)
    group = math.gcd(peers, 4)
    for at in range(0, peers, group):
        span = slice(at * n, (at + group) * n)

        def stat_rows(kind):
            heads = []
            for h in range(HEADS):
                parts = [stats[t, kind : kind + 1, h * n : (h + 1) * n] for t in range(at, at + group)]
                heads.append(jnp.broadcast_to(jnp.concatenate(parts, axis=1), (n, group * n)))
            return jnp.concatenate(heads, axis=0)

        prob_t = jnp.exp(st_buf[:, span] - stat_rows(0))
        dscore_t = (prob_t * (dpt_buf[:, span] - stat_rows(1))).astype(jnp.bfloat16)
        dv = dv + mm(prob_t.astype(jnp.bfloat16), d_all[span, :])
        dk = dk + mm(dscore_t, q_all[span, :])
    dkeys = pick_heads(dk).astype(jnp.bfloat16)
    dvalues = pick_heads(dv).astype(jnp.bfloat16)
    grad_h = grad_h + mm(dkeys, qk[1], NT) + mm(dvalues, vw[...], NT)
    dhidden = grad_h.astype(jnp.bfloat16)
    dh_all[mine, :] = dhidden
    dh_gather.own()
    parts[1].over()
    parts[2].across()
    parts[3].own()

    def back_row(a, grads):
        even = mm(grads, conv[a, 1], NT)
        later = mm(grads, conv[a, 0], NT)
        later = jnp.where(row_at == n - 1, 0.0, pltpu.roll(later, n - 1, 0))
        return even, mm(grads, conv[a, 2], NT) + later

    even_mid, odd_mid = back_row(1, dhidden)
    grad_fine[0, :, :chans] = even_mid.astype(jnp.bfloat16)
    grad_fine[0, :, chans:] = odd_mid.astype(jnp.bfloat16)
    even_low, odd_low = back_row(2, dhidden)
    dh_gather.across()
    parts[3].across()
    dh_gather.over()
    parts[2].over()
    dh_gather.finish()
    below = dh_all[pl.ds(pl.multiple_of(lower * n, n), n), :]
    below = jnp.where(me == peers - 1, jnp.zeros_like(below), below)
    even_top, odd_top = back_row(0, below)
    grad_fine[1, :, :chans] = (even_low + even_top).astype(jnp.bfloat16)
    grad_fine[1, :, chans:] = (odd_low + odd_top).astype(jnp.bfloat16)
    for t in range(peers):
        span = slice(t * n, (t + 1) * n)
        moved = pltpu.roll(dh_all[span, :].astype(jnp.float32), n - 1, 0)
        shift_all[span, :] = jnp.where(row_at == n - 1, 0.0, moved).astype(jnp.bfloat16)
    store(grad_fine, grad_fine_hbm)
    norm = 1.0 / math.sqrt(full)

    def taps(features, count):
        return jnp.concatenate([fine_t[t, features, :] for t in range(count)], axis=1)

    def finish_tap(a, b):
        source = dh_all if b else shift_all
        at = (2 if a != 1 else 0) * chans + (0 if b == 1 else chans)
        features = slice(at, at + chans)
        if a == 0:
            part = mm(taps(features, peers - 1), source[n:, :])
        else:
            part = mm(taps(features, peers), source[...])
        grad_conv[3 * a + b] = part * norm
        store(grad_conv.at[3 * a + b], grad_conv_hbm.at[3 * a + b])

    parts[0].finish()
    finish_tap(1, 1)
    parts[1].finish()
    finish_tap(1, 2)
    parts[3].over()
    finish_tap(1, 0)
    parts[2].finish()
    for a in (2, 0):
        for b in (2, 0):
            finish_tap(a, b)
    parts[3].finish()
    for a in (2, 0):
        finish_tap(a, 1)
    halo.wait_send()
    for gather in (*parts, hid_gather, d_gather, dh_gather):
        gather.drain()
    for made in stat_copies:
        made.wait_send()
    for made in stores:
        made.wait()


def fused_body(fine, conv_weight, qk_weight, v_weight, o_weight, upstream):
    peers = lax.axis_size("tile")
    n, chans = upstream.shape
    full = n * peers
    pairs = fine.reshape(2, n, 2 * chans)
    hbm = pl.BlockSpec(memory_space=pl.ANY)
    dma = pltpu.SemaphoreType.DMA
    block_out, grad_conv, grad_fine = pl.pallas_call(
        functools.partial(fused_kernel, peers),
        out_shape=(
            jax.ShapeDtypeStruct((n, chans), jnp.bfloat16),
            jax.ShapeDtypeStruct((9, chans, chans), jnp.float32),
            jax.ShapeDtypeStruct((2, n, 2 * chans), jnp.bfloat16),
        ),
        in_specs=[hbm] * 6,
        out_specs=(hbm, hbm, hbm),
        scratch_shapes=[
            pltpu.VMEM(pairs.shape, jnp.bfloat16),
            pltpu.VMEM(conv_weight.shape, jnp.bfloat16),
            pltpu.VMEM(qk_weight.shape, jnp.bfloat16),
            pltpu.VMEM(v_weight.shape, jnp.bfloat16),
            pltpu.VMEM(o_weight.shape, jnp.bfloat16),
            pltpu.VMEM(upstream.shape, jnp.bfloat16),
            pltpu.VMEM((n, chans), jnp.bfloat16),
            pltpu.VMEM((9, chans, chans), jnp.float32),
            pltpu.VMEM((2, n, 2 * chans), jnp.bfloat16),
            dma((6,)),
            dma((11,)),
            pltpu.VMEM((n, 2 * chans), jnp.bfloat16),
            pltpu.VMEM((full, chans), jnp.bfloat16),
            pltpu.VMEM((full, 2 * HD), jnp.bfloat16),
            pltpu.VMEM((full, HD), jnp.bfloat16),
            pltpu.VMEM((full, HD), jnp.bfloat16),
            pltpu.VMEM((full, chans), jnp.bfloat16),
            pltpu.VMEM((full, chans), jnp.bfloat16),
            pltpu.VMEM((peers, 4 * chans, n), jnp.bfloat16),
            pltpu.VMEM((peers, 2, 2 * n), jnp.float32),
            pltpu.VMEM((2 * n, full), jnp.float32),
            pltpu.VMEM((2 * n, full), jnp.float32),
            dma((7, peers)),
            dma((7, peers)),
            dma((peers,)),
            dma((peers,)),
            dma,
            dma,
        ],
        compiler_params=pltpu.CompilerParams(
            collective_id=0, has_side_effects=True, vmem_limit_bytes=60 * 2**20
        ),
    )(pairs, conv_weight, qk_weight, v_weight, o_weight, upstream)
    return (
        block_out,
        grad_conv.reshape(3, 3, chans, chans),
        grad_fine.reshape(fine.shape),
    )


def solution(mesh):
    def whole(fine, *rest):
        devices = mesh.shape["groups"] * mesh.shape["tile"]
        one_row = fine.shape[0] == 2 * devices and fine.shape[1] == 256 and fine.shape[2] == 256
        fits = fine.size // mesh.shape["groups"] <= 4 * 2**20 and mesh.shape["tile"] % 4 == 0
        return jax.shard_map(
            fused_body if one_row and fits else body,
            mesh=mesh,
            in_specs=(
                P(("groups", "tile"), None, None),
                P(),
                P(),
                P(),
                P(),
                P(("groups", "tile"), None),
            ),
            out_specs=(
                P(("groups", "tile"), None),
                P("groups", None, None, None),
                P(("groups", "tile"), None, None),
            ),
            check_vma=False,
        )(fine, *rest)

    return whole
```
